32 devices in a mesh: groups: 2 (over y), tm: 4 (over z), lat: 2 (over x), lon: 2 (over core).
Axes of the slice: x: 2, y: 2, z: 4, core: 2. Of those that a mesh axis runs over, the one named last changes fastest.
Arguments:
- prior_state: float32 [16, 8, 16, 256], P(('groups', 'tm'), None, 'lat', 'lon'), parts along dimension 0, may hold values from -6 to 6
- observed: float32 [16, 8, 16, 256], P(('groups', 'tm'), None, 'lat', 'lon'), parts along dimension 0, may hold values from -6 to 6
- obs_weight: float32 [16, 8, 16, 256], P(('groups', 'tm'), None, 'lat', 'lon'), parts along dimension 0, may hold values from 0 to 2
- noise_field: float32 [2, 16, 8, 16, 256], P(None, ('groups', 'tm'), None, 'lat', 'lon'), parts along dimension 1, may hold values from -6 to 6
- step_sizes: float32 [2], replicated, may hold values from 0.05 to 0.3
- lift_weight: float32 [96, 40], replicated, may hold values from -1 to 1
- conv_weights: bfloat16 [2, 9, 96, 96], replicated, may hold values from -0.21875 to 0.21875
- out_weight: bfloat16 [8, 96], replicated, may hold values from -0.625 to 0.625
Outputs:
- analysis: float32 [16, 8, 16, 256], P(('groups', 'tm'), None, 'lat', 'lon'), parts along dimension 0
The draws below stay inside these ranges and needn't reach their ends.
There are 2 independent parts, one for each index of `groups`. The reference program is written for one: setup_inputs(seed, part) draws one part's arguments, and reference() takes and returns one part's arrays. A program takes and returns all parts, laid end to end along the dimension named above; an argument that names none is the same for every part. Nothing has to cross between parts.
All inputs are finite; a program needn't handle non-finite values.
Results may differ from the reference program's by a relative error of at most 0.0012.
Values may be sent and summed in bfloat16 or wider, within the bound.
No kernel may reach another device: no remote copies, remote signals or barrier semaphores. Data moves between devices by JAX's collectives and lax.ppermute only.
A program may use at most 64 MiB of HBM per device.

```python
import math
import jax
import jax.numpy as jnp
from jax import lax

C = 8
HIDDEN_SIZE = 96
STACK = 5
STEPS = 2
FRAMES = 8
LAT = 16
LON = 256


def block_scale(stream_key, dims, shards, least, high):
    factor_of, own = 1.0, jax.random.fold_in(stream_key, 6)
    for position, blocks in shards:
        draws = jnp.exp(jax.random.uniform(jax.random.fold_in(own, position), (blocks,), jnp.float32, least / len(shards), high / len(shards)))
        factor_of = factor_of * jnp.repeat(draws, dims[position] // blocks).reshape([-1 if axis == position else 1 for axis in range(len(dims))])
    return factor_of


def normal_values(stream_key, extent, spread, most, shards=(), kind=jnp.bfloat16):
    factor_of = block_scale(stream_key, extent, shards, -0.22, 0.18) if shards else 1.0
    array = jax.random.normal(stream_key, extent, jnp.float32) * spread * factor_of
    return jnp.minimum(jnp.maximum(array, -most), most).astype(kind)


def setup_inputs(seed: int = 0, part: int = 0) -> dict:
    seeds = jax.random.split(jax.random.key(seed), 9)
    part_splits = jax.random.split(jax.random.fold_in(seeds[8], part), 9)
    prior_state = normal_values(part_splits[0], (FRAMES, C, LAT, LON), 1.0, 6.0, ((0, 4), (2, 2), (3, 2)), jnp.float32)
    observed = normal_values(part_splits[1], (FRAMES, C, LAT, LON), 1.0, 6.0, ((0, 4), (2, 2), (3, 2)), jnp.float32)
    obs_weight = jnp.clip(2.0 * jax.random.uniform(part_splits[2], (FRAMES, C, LAT, LON), jnp.float32) ** block_scale(part_splits[2], (FRAMES, C, LAT, LON), ((0, 4), (2, 2), (3, 2)), -0.2, 0.2), 0.0, 2.0)
    noise_field = normal_values(part_splits[3], (STEPS, FRAMES, C, LAT, LON), 1.0, 6.0, ((1, 4), (3, 2), (4, 2)), jnp.float32)
    step_sizes = jnp.clip(jnp.exp(jax.random.uniform(seeds[4], (STEPS,), jnp.float32, math.log(0.05), math.log(0.3))), 0.05, 0.3)
    lift_weight = normal_values(seeds[5], (HIDDEN_SIZE, STACK * C), (STACK * C) ** -0.5, 1.0, (), jnp.float32)
    conv_weights = normal_values(seeds[6], (2, 9, HIDDEN_SIZE, HIDDEN_SIZE), (9 * HIDDEN_SIZE) ** -0.5, 0.21875)
    out_weight = normal_values(seeds[7], (C, HIDDEN_SIZE), HIDDEN_SIZE ** -0.5, 0.625)
    return dict(prior_state=prior_state, observed=observed, obs_weight=obs_weight, noise_field=noise_field, step_sizes=step_sizes, lift_weight=lift_weight, conv_weights=conv_weights, out_weight=out_weight)


def conv_layer(values, kernel):
    height = values.shape[1]
    width = values.shape[2]
    padded = jnp.pad(values, ((0, 0), (1, 1), (0, 0)))
    padded = jnp.concatenate([padded[:, :, -1:], padded, padded[:, :, :1]], axis=2)
    summed = jnp.zeros((kernel.shape[1], height, width), jnp.float32)
    for row_off in range(3):
        for col_off in range(3):
            tap = kernel[3 * row_off + col_off].astype(jnp.float32)
            part = padded[:, row_off:row_off + height, col_off:col_off + width].astype(jnp.float32)
            summed = summed + jnp.einsum('oi,ihw->ohw', tap, part)
    return summed

def score_all(current, lift_weight, conv_weights, out_weight):
    height = current.shape[2]
    width = current.shape[3]
    padded = jnp.pad(current, ((2, 2), (0, 0), (0, 0), (0, 0)))

    def frame_score(frame_index):
        window = lax.dynamic_slice_in_dim(padded, frame_index, 5, 0)
        stacked = window.reshape(-1, height, width)
        lifted = jnp.einsum('oc,chw->ohw', lift_weight, stacked, precision=lax.Precision.HIGHEST).astype(jnp.bfloat16)
        activated = jax.nn.silu(conv_layer(lifted, conv_weights[0])).astype(jnp.bfloat16)
        second = jax.nn.silu(conv_layer(activated, conv_weights[1]))
        merged = (lifted.astype(jnp.float32) + second).astype(jnp.bfloat16)
        return jnp.einsum('co,ohw->chw', out_weight.astype(jnp.float32), merged.astype(jnp.float32))
    return lax.map(frame_score, jnp.arange(current.shape[0], dtype=jnp.int32))

def reference(prior_state, observed, obs_weight, noise_field, step_sizes, lift_weight, conv_weights, out_weight):
    current = prior_state
    for update in range(noise_field.shape[0]):
        step_size = step_sizes[update]
        score = score_all(current, lift_weight, conv_weights, out_weight)
        current = current + step_size * (score + obs_weight * (observed - current)) + jnp.sqrt(2.0 * step_size) * noise_field[update]
    return current
```

```python
import functools

import jax
import jax.numpy as jnp
from jax import lax
from jax.experimental import pallas as pl
from jax.experimental.pallas import tpu as pltpu
from jax.sharding import PartitionSpec as P

LANES = 128
REACH = 4
EDGE = 2 * REACH
BF = jnp.bfloat16
F32 = jnp.float32


def ring_edges(rows_of, rows, first, count, lanes):
    lane = lax.broadcasted_iota(jnp.int32, rows_of(0).shape, 1)
    tile = jnp.zeros(rows_of(0).shape, F32)
    for row in range(count):
        at = first + EDGE * row
        value = rows_of(rows + row)
        low = pltpu.roll(value, at % lanes, 1)
        high = pltpu.roll(value, (at + EDGE) % lanes, 1)
        tile = jnp.where((lane >= at) & (lane < at + REACH), low, tile)
        tile = jnp.where((lane >= at + REACH) & (lane < at + EDGE), high, tile)
    return tile


def pack_kernel(
    geometry, step_ref, prior, observed, weight, noise,
    state_out, base_out, lon_out, down_rows, down_edge, up_rows, up_edge, state, base,
):
    frames, chans, rows = geometry
    step = step_ref[0]
    spread = jnp.sqrt(jnp.full((chans, LANES), 2.0 * step, F32))
    for row in range(rows):
        for frame in range(frames):
            part = pl.ds(frame * chans * rows + row, chans, stride=rows)
            own = prior[part, :]
            state[row, frame * chans : (frame + 1) * chans, :] = own
            base[row, frame * chans : (frame + 1) * chans, :] = (
                own + step * (weight[part, :] * (observed[part, :] - own)) + spread * noise[part, :]
            )
    for row in range(rows):
        state_out[row] = state[row].astype(BF)
        base_out[row] = base[row]
    lon_out[0] = ring_edges(lambda r: state[r], 0, EDGE * REACH, rows, LANES).astype(BF)
    lon_out[1] = ring_edges(lambda r: base[r], 0, EDGE * 2, rows, LANES).astype(BF)
    for out, edge, start, at in (
        (down_rows, down_edge, rows - REACH, 0),
        (up_rows, up_edge, 0, rows + REACH),
    ):
        skip = start + 2 if at == 0 else start
        at_base = 0 if at == 0 else rows + 2
        for row in range(REACH):
            out[row] = state[start + row].astype(BF)
        for row in range(2):
            out[REACH + row] = base[skip + row].astype(BF)
        edge[0] = ring_edges(lambda r: state[r], start, EDGE * at, REACH, LANES).astype(BF)
        edge[1] = ring_edges(lambda r: base[r], skip, EDGE * at_base, 2, LANES).astype(BF)


def features(geometry, in_rows, own, prev, following, lift, act, halo):
    frames, ring = geometry
    dims = (((0,), (0,)), ((), ()))

    def lifted(tile):
        stacked = jnp.concatenate([prev[tile], own[tile], following[tile]], axis=0)
        turned = jnp.transpose(stacked.astype(F32)).astype(BF)
        return jnp.dot(turned, lift[0], preferred_element_type=F32) + jnp.dot(
            turned, lift[1], preferred_element_type=F32
        )

    halo[...] = lifted(in_rows)
    for row in range(in_rows):
        main = lifted(row)
        whole = jnp.concatenate([main, halo[row * EDGE : (row + 1) * EDGE, :]], axis=0)
        for frame in range(frames):
            store_shifts(act, frame, row, ring, whole[:, frame * LANES : (frame + 1) * LANES])


def store_shifts(act, frame, row, ring, value):
    act[0, frame, row, :ring, :] = pltpu.roll(value, 1, 0).astype(BF)
    act[1, frame, row, :ring, :] = value.astype(BF)
    act[2, frame, row, :ring, :] = pltpu.roll(value, ring - 1, 0).astype(BF)


def conv_pairs(act, frame, weight, first, count):
    pieces = [
        jnp.concatenate([act[col, frame, 2 * (first + p) + row] for p in range(count)], axis=0)
        for row in range(4)
        for col in range(3)
    ]
    return jnp.dot(jnp.concatenate(pieces, axis=1), weight[...], preferred_element_type=F32)


def gated(half):
    return half + half * jnp.tanh(half)


def convolve(geometry, in_rows, reach, act, act2, sums, conv_a, conv_b, top, bottom, emit):
    frames, ring, pad, chunk = geometry
    for frame in range(frames):
        pairs = (in_rows - 2) // 2
        for first in range(0, pairs, chunk):
            count = min(chunk, pairs - first)
            sums[: count * pad, :] = conv_pairs(act, frame, conv_a, first, count)
            for p in range(count):
                for q in range(2):
                    row = 1 + 2 * (first + p) + q
                    value = gated(sums[p * pad : p * pad + ring, q * LANES : (q + 1) * LANES])
                    if row < reach:
                        value = value * top
                    if row >= in_rows - reach:
                        value = value * bottom
                    store_shifts(act2, frame, row - 1, ring, value)
        pairs = (in_rows - 4) // 2
        for first in range(0, pairs, chunk):
            count = min(chunk, pairs - first)
            sums[: count * pad, :] = conv_pairs(act2, frame, conv_b, first, count)
            for p in range(count):
                for q in range(2):
                    row = 2 + 2 * (first + p) + q
                    value = gated(sums[p * pad : p * pad + ring, q * LANES : (q + 1) * LANES])
                    merged = act[1, frame, row, :ring, :].astype(F32) + value
                    emit(frame, row - 2, merged)


def edge_flags():
    lat = lax.axis_index("lat")
    top = jnp.where(lat > 0, 1.0, 0.0).astype(F32)
    bottom = jnp.where(lat < lax.axis_size("lat") - 1, 1.0, 0.0).astype(F32)
    return top, bottom


def project(out_weight, merged):
    return lax.dot_general(
        out_weight[...], merged, (((1,), (1,)), ((), ())), preferred_element_type=F32
    )


def first_kernel(
    geometry, step_ref, own, prev, following, base, base_edge, lift, conv_a, conv_b, out_weight,
    next_out, state_out, act, act2, sums, halo, halo_merged,
):
    frames, chans, rows, ring, pad, chunk = geometry
    in_rows, out_rows = rows + 2 * REACH, rows + 4
    top, bottom = edge_flags()
    step = step_ref[0]
    features((frames, ring), in_rows, own, prev, following, lift, act, halo)

    def emit(frame, row, merged):
        score = project(out_weight, merged[:LANES].astype(BF))
        part = slice(frame * chans, (frame + 1) * chans)
        if row < 2:
            start = base_edge[row, part, :].astype(F32)
        elif row < rows + 2:
            start = base[row - 2, part, :]
        else:
            start = base_edge[row - rows, part, :].astype(F32)
        value = start + step * score
        if row < 2:
            value = value * top
        if row >= rows + 2:
            value = value * bottom
        state_out[row, part, :] = value
        halo_merged[frame, row * EDGE : (row + 1) * EDGE, :] = merged[LANES:]

    convolve(
        (frames, ring, pad, chunk), in_rows, REACH, act, act2, sums, conv_a, conv_b, top, bottom, emit
    )
    for row in range(out_rows):
        next_out[row] = state_out[row].astype(BF)
    edges = [project(out_weight, halo_merged[frame].astype(BF)) for frame in range(frames)]
    score = jnp.concatenate(edges, axis=0)
    value = base_edge[4].astype(F32) + step * score
    lane = lax.broadcasted_iota(jnp.int32, value.shape, 1)
    value = jnp.where(lane < 2 * EDGE, value * top, value)
    value = jnp.where(lane >= (rows + 2) * EDGE, value * bottom, value)
    value = jnp.where(lane < out_rows * EDGE, value, 0.0)
    next_out[out_rows] = value.astype(BF)


def last_kernel(
    geometry, step_ref, own, prev, following, state, observed, weight, noise, lift, conv_a, conv_b,
    out_weight, result, act, act2, sums, halo,
):
    frames, chans, rows, ring, pad, chunk = geometry
    in_rows = rows + 4
    top, bottom = edge_flags()
    step = step_ref[1]
    spread = jnp.sqrt(jnp.full((chans, LANES), 2.0 * step, F32))
    features((frames, ring), in_rows, own, prev, following, lift, act, halo)

    def emit(frame, row, merged):
        score = project(out_weight, merged[:LANES].astype(BF))
        part = pl.ds(frame * chans * rows + row, chans, stride=rows)
        before = state[row + 2, frame * chans : (frame + 1) * chans, :]
        result[part, :] = (
            before
            + step * (score + weight[part, :] * (observed[part, :] - before))
            + spread * noise[part, :]
        )

    convolve((frames, ring, pad, chunk), in_rows, 2, act, act2, sums, conv_a, conv_b, top, bottom, emit)


def ring_perm(count, by):
    return [(i, (i + by) % count) for i in range(count)]


def lane_weights(lift_weight, conv_weights, out_weight):
    hidden, stacked = lift_weight.shape
    gap = LANES - hidden
    chans = out_weight.shape[0]
    turned = lift_weight.T
    lanes = [
        jnp.pad(turned, ((frame * chans, (1 - frame) * chans), (0, gap))) for frame in range(2)
    ]
    lift = jnp.concatenate(lanes, axis=1)
    block = 2 * chans
    tm = lax.axis_index("tm")
    kept = jnp.concatenate(
        [
            jnp.full((block, 1), jnp.where(tm > 0, 1.0, 0.0), F32),
            jnp.ones((block, 1), F32),
            jnp.full((block, 1), jnp.where(tm < lax.axis_size("tm") - 1, 1.0, 0.0), F32),
        ],
        axis=0,
    )
    lift = lift * kept
    high = lax.reduce_precision(lift, 8, 7)
    lift = jnp.stack([high.astype(BF), (lift - high).astype(BF)])
    half = conv_weights * jnp.asarray(0.5, BF)
    taps = jnp.swapaxes(half, 2, 3).reshape(2, 3, 3, hidden, hidden)
    taps = jnp.pad(taps, ((0, 0), (0, 0), (0, 0), (0, gap), (0, gap)))
    pair = jnp.concatenate(
        [
            jnp.pad(taps, ((0, 0), (0, 1), (0, 0), (0, 0), (0, 0))),
            jnp.pad(taps, ((0, 0), (1, 0), (0, 0), (0, 0), (0, 0))),
        ],
        axis=4,
    )
    conv = pair.reshape(2, 12 * LANES, 2 * LANES)
    return lift, conv[0], conv[1], jnp.pad(out_weight, ((0, 0), (0, gap)))


def per_device(
    prior_state, observed, obs_weight, noise_field, step_sizes, lift_weight, conv_weights, out_weight
):
    frames, chans, rows, cols = prior_state.shape
    lat_count, lon_count = lax.axis_size("lat"), lax.axis_size("lon")
    fc = frames * chans
    ring, pad, chunk = cols + EDGE, cols + 16, 4
    smem = pl.BlockSpec(memory_space=pltpu.SMEM)
    vmem = pl.BlockSpec(memory_space=pltpu.VMEM)
    shape = jax.ShapeDtypeStruct
    flat = lambda array: array.reshape(fc * rows, cols)

    packed = pl.pallas_call(
        functools.partial(pack_kernel, (frames, chans, rows)),
        out_shape=(
            shape((rows, fc, cols), BF),
            shape((rows, fc, cols), F32),
            shape((2, fc, cols), BF),
            shape((REACH + 2, fc, cols), BF),
            shape((2, fc, cols), BF),
            shape((REACH + 2, fc, cols), BF),
            shape((2, fc, cols), BF),
        ),
        in_specs=[smem] + [vmem] * 4,
        out_specs=[vmem] * 7,
        scratch_shapes=[pltpu.VMEM((rows, fc, cols), F32), pltpu.VMEM((rows, fc, cols), F32)],
    )(step_sizes, flat(prior_state), flat(observed), flat(obs_weight), flat(noise_field[0]))
    state, base, lon_edge, down_rows, down_edge, up_rows, up_edge = packed

    lat = lax.axis_index("lat")
    spot = ("lat", "lon")

    def lon_pick(array, axes, lat_shift):
        def move(by):
            perm = []
            for a in range(lat_count):
                for o in range(lon_count):
                    b = (a + lat_shift) % lat_count
                    perm.append((a * lon_count + o, b * lon_count + (o + by) % lon_count))
            return lax.ppermute(array, spot, perm)

        if lon_count <= 2:
            return move(lon_count - 1)
        lane = lax.broadcasted_iota(jnp.int32, array.shape, array.ndim - 1)
        return jnp.where(lane % EDGE < REACH, move(-1), move(1))

    has_top, has_bottom = lat > 0, lat < lat_count - 1
    side = lon_pick(lon_edge, spot, 0)
    if lat_count == 2:
        rows_in = lax.ppermute(jnp.where(has_top, up_rows, down_rows), "lat", ring_perm(2, 1))
        corner = lon_pick(jnp.where(has_top, up_edge, down_edge), spot, 1)
        from_top, from_bottom = rows_in, rows_in
        edge = side + corner
    else:
        from_top = lax.ppermute(down_rows, "lat", ring_perm(lat_count, 1))
        from_bottom = lax.ppermute(up_rows, "lat", ring_perm(lat_count, -1))
        zero = jnp.zeros_like(side)
        edge = (
            side
            + jnp.where(has_top, lon_pick(down_edge, spot, 1), zero)
            + jnp.where(has_bottom, lon_pick(up_edge, spot, -1), zero)
        )
    from_top = jnp.where(has_top, from_top, jnp.zeros_like(from_top))
    from_bottom = jnp.where(has_bottom, from_bottom, jnp.zeros_like(from_bottom))
    own = jnp.concatenate([from_top[:REACH], state, from_bottom[:REACH], edge[:1]], axis=0)
    base_edge = jnp.concatenate([from_top[REACH:], from_bottom[REACH:], edge[1:]], axis=0)

    lift, conv_a, conv_b, out_lanes = lane_weights(lift_weight, conv_weights, out_weight)
    tm_count = lax.axis_size("tm")

    def neighbours(array):
        return (
            lax.ppermute(array, "tm", ring_perm(tm_count, 1)),
            lax.ppermute(array, "tm", ring_perm(tm_count, -1)),
        )

    geometry = (frames, chans, rows, ring, pad, chunk)

    def scratch(in_rows):
        return [
            pltpu.VMEM((3, frames, in_rows, pad, LANES), BF),
            pltpu.VMEM((3, frames, in_rows - 2, pad, LANES), BF),
            pltpu.VMEM((chunk * pad, 2 * LANES), F32),
            pltpu.VMEM((LANES, 2 * LANES), F32),
        ]

    prev, following = neighbours(own)
    nxt, current = pl.pallas_call(
        functools.partial(first_kernel, geometry),
        out_shape=(shape((rows + 5, fc, cols), BF), shape((rows + 4, fc, cols), F32)),
        in_specs=[smem] + [vmem] * 9,
        out_specs=[vmem] * 2,
        scratch_shapes=scratch(rows + 2 * REACH) + [pltpu.VMEM((frames, LANES, LANES), F32)],
    )(step_sizes, own, prev, following, base, base_edge, lift, conv_a, conv_b, out_lanes)

    prev, following = neighbours(nxt)
    result = pl.pallas_call(
        functools.partial(last_kernel, geometry),
        out_shape=shape((fc * rows, cols), F32),
        in_specs=[smem] + [vmem] * 11,
        out_specs=vmem,
        scratch_shapes=scratch(rows + 4),
    )(
        step_sizes, nxt, prev, following, current, flat(observed), flat(obs_weight),
        flat(noise_field[1]), lift, conv_a, conv_b, out_lanes,
    )
    return result.reshape(prior_state.shape)


def solution(mesh):
    placed = (
        P(("groups", "tm"), None, "lat", "lon"),
        P(("groups", "tm"), None, "lat", "lon"),
        P(("groups", "tm"), None, "lat", "lon"),
        P(None, ("groups", "tm"), None, "lat", "lon"),
        P(),
        P(),
        P(),
        P(),
    )
    return jax.shard_map(
        per_device,
        mesh=mesh,
        in_specs=placed,
        out_specs=P(("groups", "tm"), None, "lat", "lon"),
        check_vma=False,
    )
```

```python
import functools

import jax
import jax.numpy as jnp
from jax import lax
from jax.experimental import pallas as pl
from jax.experimental.pallas import tpu as pltpu
from jax.sharding import PartitionSpec as P

LANES = 128
REACH = 4
EDGE = 2 * REACH
GRANT = 24 << 20
BF = jnp.bfloat16
F32 = jnp.float32


def ring_edges(rows_of, rows, first, count, lanes):
    lane = lax.broadcasted_iota(jnp.int32, rows_of(0).shape, 1)
    tile = jnp.zeros(rows_of(0).shape, F32)
    for row in range(count):
        at = first + EDGE * row
        value = rows_of(rows + row)
        low = pltpu.roll(value, at % lanes, 1)
        high = pltpu.roll(value, (at + EDGE) % lanes, 1)
        tile = jnp.where((lane >= at) & (lane < at + REACH), low, tile)
        tile = jnp.where((lane >= at + REACH) & (lane < at + EDGE), high, tile)
    return tile


def pack_kernel(
    geometry, step_ref, prior, observed, weight, noise,
    state_out, base_out, lon_out, *rest,
):
    frames, chans, rows, single = geometry
    *outs, state, base = rest
    step = step_ref[0]
    spread = jnp.sqrt(jnp.full((chans, LANES), 2.0 * step, F32))
    for row in range(rows):
        for frame in range(frames):
            part = pl.ds(frame * chans * rows + row, chans, stride=rows)
            own = prior[part, :]
            state[row, frame * chans : (frame + 1) * chans, :] = own
            base[row, frame * chans : (frame + 1) * chans, :] = (
                own + step * (weight[part, :] * (observed[part, :] - own)) + spread * noise[part, :]
            )
    for row in range(rows):
        state_out[row] = state[row].astype(BF)
        base_out[row] = base[row]
    lon_out[0] = ring_edges(lambda r: state[r], 0, EDGE * REACH, rows, LANES).astype(BF)
    lon_out[1] = ring_edges(lambda r: base[r], 0, EDGE * 2, rows, LANES).astype(BF)
    sides = []
    for start, at in ((rows - REACH, 0), (0, rows + REACH)):
        skip = start + 2 if at == 0 else start
        at_base = 0 if at == 0 else rows + 2
        tiles = [state[start + row] for row in range(REACH)] + [base[skip + row] for row in range(2)]
        tiles.append(ring_edges(lambda r: state[r], start, EDGE * at, REACH, LANES))
        tiles.append(ring_edges(lambda r: base[r], skip, EDGE * at_base, 2, LANES))
        sides.append(tiles)
    if single:
        upward = lax.axis_index("lat") > 0
        sides = [[jnp.where(upward, up, down) for down, up in zip(*sides)]]
    for tiles, rows_out, edge_out in zip(sides, outs[::2], outs[1::2]):
        for place, tile in enumerate(tiles[: REACH + 2]):
            rows_out[place] = tile.astype(BF)
        for place, tile in enumerate(tiles[REACH + 2 :]):
            edge_out[place] = tile.astype(BF)


def features(geometry, in_rows, own, prev, following, lift, act, halo):
    frames, ring = geometry
    dims = (((0,), (0,)), ((), ()))

    def lifted(tile):
        stacked = jnp.concatenate([prev[tile], own[tile], following[tile]], axis=0)
        turned = jnp.transpose(stacked.astype(F32)).astype(BF)
        return jnp.dot(turned, lift[0], preferred_element_type=F32) + jnp.dot(
            turned, lift[1], preferred_element_type=F32
        )

    halo[...] = lifted(in_rows)
    for row in range(in_rows):
        main = lifted(row)
        whole = jnp.concatenate([main, halo[row * EDGE : (row + 1) * EDGE, :]], axis=0)
        for frame in range(frames):
            store_shifts(act, frame, row, ring, whole[:, frame * LANES : (frame + 1) * LANES])


def store_shifts(act, frame, row, ring, value):
    act[0, frame, row, :ring, :] = pltpu.roll(value, 1, 0).astype(BF)
    act[1, frame, row, :ring, :] = value.astype(BF)
    act[2, frame, row, :ring, :] = pltpu.roll(value, ring - 1, 0).astype(BF)


def conv_pairs(act, frame, weight, first, count):
    pieces = [
        jnp.concatenate([act[col, frame, 2 * (first + p) + row] for p in range(count)], axis=0)
        for row in range(4)
        for col in range(3)
    ]
    return jnp.dot(jnp.concatenate(pieces, axis=1), weight[...], preferred_element_type=F32)


def gated(half):
    return half + half * jnp.tanh(half)


def convolve(geometry, in_rows, reach, act, act2, sums, conv_a, conv_b, top, bottom, emit):
    frames, ring, pad, chunk = geometry
    for frame in range(frames):
        pairs = (in_rows - 2) // 2
        for first in range(0, pairs, chunk):
            count = min(chunk, pairs - first)
            sums[: count * pad, :] = conv_pairs(act, frame, conv_a, first, count)
            for p in range(count):
                for q in range(2):
                    row = 1 + 2 * (first + p) + q
                    value = gated(sums[p * pad : p * pad + ring, q * LANES : (q + 1) * LANES])
                    if row < reach:
                        value = value * top
                    if row >= in_rows - reach:
                        value = value * bottom
                    store_shifts(act2, frame, row - 1, ring, value)
        pairs = (in_rows - 4) // 2
        for first in range(0, pairs, chunk):
            count = min(chunk, pairs - first)
            sums[: count * pad, :] = conv_pairs(act2, frame, conv_b, first, count)
            for p in range(count):
                for q in range(2):
                    row = 2 + 2 * (first + p) + q
                    value = gated(sums[p * pad : p * pad + ring, q * LANES : (q + 1) * LANES])
                    merged = act[1, frame, row, :ring, :].astype(F32) + value
                    emit(frame, row - 2, merged)


def edge_flags():
    lat = lax.axis_index("lat")
    top = jnp.where(lat > 0, 1.0, 0.0).astype(F32)
    bottom = jnp.where(lat < lax.axis_size("lat") - 1, 1.0, 0.0).astype(F32)
    return top, bottom


def project(out_weight, merged):
    return lax.dot_general(
        out_weight[...], merged, (((1,), (1,)), ((), ())), preferred_element_type=F32
    )


def first_kernel(
    geometry, step_ref, own, prev, following, base, base_edge, lift, conv_a, conv_b, out_weight,
    next_out, state_out, act, act2, sums, halo, halo_merged,
):
    frames, chans, rows, ring, pad, chunk = geometry
    in_rows, out_rows = rows + 2 * REACH, rows + 4
    top, bottom = edge_flags()
    step = step_ref[0]
    features((frames, ring), in_rows, own, prev, following, lift, act, halo)

    def emit(frame, row, merged):
        score = project(out_weight, merged[:LANES].astype(BF))
        part = slice(frame * chans, (frame + 1) * chans)
        if row < 2:
            start = base_edge[row, part, :].astype(F32)
        elif row < rows + 2:
            start = base[row - 2, part, :]
        else:
            start = base_edge[row - rows, part, :].astype(F32)
        value = start + step * score
        if row < 2:
            value = value * top
        if row >= rows + 2:
            value = value * bottom
        state_out[row, part, :] = value
        halo_merged[frame, row * EDGE : (row + 1) * EDGE, :] = merged[LANES:]

    convolve(
        (frames, ring, pad, chunk), in_rows, REACH, act, act2, sums, conv_a, conv_b, top, bottom, emit
    )
    for row in range(out_rows):
        next_out[row] = state_out[row].astype(BF)
    edges = [project(out_weight, halo_merged[frame].astype(BF)) for frame in range(frames)]
    score = jnp.concatenate(edges, axis=0)
    value = base_edge[4].astype(F32) + step * score
    lane = lax.broadcasted_iota(jnp.int32, value.shape, 1)
    value = jnp.where(lane < 2 * EDGE, value * top, value)
    value = jnp.where(lane >= (rows + 2) * EDGE, value * bottom, value)
    value = jnp.where(lane < out_rows * EDGE, value, 0.0)
    next_out[out_rows] = value.astype(BF)


def last_kernel(
    geometry, step_ref, own, prev, following, state, observed, weight, noise, lift, conv_a, conv_b,
    out_weight, result, act, act2, sums, halo,
):
    frames, chans, rows, ring, pad, chunk = geometry
    in_rows = rows + 4
    top, bottom = edge_flags()
    step = step_ref[1]
    spread = jnp.sqrt(jnp.full((chans, LANES), 2.0 * step, F32))
    features((frames, ring), in_rows, own, prev, following, lift, act, halo)

    def emit(frame, row, merged):
        score = project(out_weight, merged[:LANES].astype(BF))
        part = pl.ds(frame * chans * rows + row, chans, stride=rows)
        late = pl.ds((frames + frame) * chans * rows + row, chans, stride=rows)
        before = state[row + 2, frame * chans : (frame + 1) * chans, :]
        result[part, :] = (
            before
            + step * (score + weight[part, :] * (observed[part, :] - before))
            + spread * noise[late, :]
        )

    convolve((frames, ring, pad, chunk), in_rows, 2, act, act2, sums, conv_a, conv_b, top, bottom, emit)


def ring_perm(count, by):
    return [(i, (i + by) % count) for i in range(count)]


def lane_weights(lift_weight, conv_weights, out_weight):
    hidden, stacked = lift_weight.shape
    gap = LANES - hidden
    chans = out_weight.shape[0]
    turned = lift_weight.T
    lanes = [
        jnp.pad(turned, ((frame * chans, (1 - frame) * chans), (0, gap))) for frame in range(2)
    ]
    lift = jnp.concatenate(lanes, axis=1)
    block = 2 * chans
    tm = lax.axis_index("tm")
    kept = jnp.concatenate(
        [
            jnp.full((block, 1), jnp.where(tm > 0, 1.0, 0.0), F32),
            jnp.ones((block, 1), F32),
            jnp.full((block, 1), jnp.where(tm < lax.axis_size("tm") - 1, 1.0, 0.0), F32),
        ],
        axis=0,
    )
    lift = lift * kept
    high = lax.reduce_precision(lift, 8, 7)
    lift = jnp.stack([high.astype(BF), (lift - high).astype(BF)])
    half = conv_weights * jnp.asarray(0.5, BF)
    taps = jnp.swapaxes(half, 2, 3).reshape(2, 3, 3, hidden, hidden)
    taps = jnp.pad(taps, ((0, 0), (0, 0), (0, 0), (0, gap), (0, gap)))
    pair = jnp.concatenate(
        [
            jnp.pad(taps, ((0, 0), (0, 1), (0, 0), (0, 0), (0, 0))),
            jnp.pad(taps, ((0, 0), (1, 0), (0, 0), (0, 0), (0, 0))),
        ],
        axis=4,
    )
    conv = pair.reshape(2, 12 * LANES, 2 * LANES)
    return lift, conv[0], conv[1], jnp.pad(out_weight, ((0, 0), (0, gap)))


def per_device(
    prior_state, observed, obs_weight, noise_field, step_sizes, lift_weight, conv_weights, out_weight
):
    frames, chans, rows, cols = prior_state.shape
    lat_count, lon_count = lax.axis_size("lat"), lax.axis_size("lon")
    fc = frames * chans
    ring, pad, chunk = cols + EDGE, cols + 16, 4
    smem = pl.BlockSpec(memory_space=pltpu.SMEM)
    vmem = pl.BlockSpec(memory_space=pltpu.VMEM)
    shape = jax.ShapeDtypeStruct
    flat = lambda array: array.reshape(fc * rows, cols)

    sides = (shape((REACH + 2, fc, cols), BF), shape((2, fc, cols), BF)) * (
        1 if lat_count == 2 else 2
    )
    state, base, lon_edge, *outward = pl.pallas_call(
        functools.partial(pack_kernel, (frames, chans, rows, lat_count == 2)),
        out_shape=(
            shape((rows, fc, cols), BF),
            shape((rows, fc, cols), F32),
            shape((2, fc, cols), BF),
            *sides,
        ),
        in_specs=[smem] + [vmem] * 4,
        out_specs=[vmem] * (3 + len(sides)),
        scratch_shapes=[pltpu.VMEM((rows, fc, cols), F32), pltpu.VMEM((rows, fc, cols), F32)],
        compiler_params=pltpu.CompilerParams(vmem_limit_bytes=GRANT),
    )(step_sizes, flat(prior_state), flat(observed), flat(obs_weight), noise_field.reshape(-1, cols))

    lat = lax.axis_index("lat")
    spot = ("lat", "lon")

    def lon_pick(array, axes, lat_shift):
        def move(by):
            perm = []
            for a in range(lat_count):
                for o in range(lon_count):
                    b = (a + lat_shift) % lat_count
                    perm.append((a * lon_count + o, b * lon_count + (o + by) % lon_count))
            return lax.ppermute(array, spot, perm)

        if lon_count <= 2:
            return move(lon_count - 1)
        lane = lax.broadcasted_iota(jnp.int32, array.shape, array.ndim - 1)
        return jnp.where(lane % EDGE < REACH, move(-1), move(1))

    has_top, has_bottom = lat > 0, lat < lat_count - 1
    side = lon_pick(lon_edge, spot, 0)
    if lat_count == 2:
        rows_in = lax.ppermute(outward[0], "lat", ring_perm(2, 1))
        corner = lon_pick(outward[1], spot, 1)
        from_top, from_bottom = rows_in, rows_in
        edge = side + corner
    else:
        down_rows, down_edge, up_rows, up_edge = outward
        from_top = lax.ppermute(down_rows, "lat", ring_perm(lat_count, 1))
        from_bottom = lax.ppermute(up_rows, "lat", ring_perm(lat_count, -1))
        zero = jnp.zeros_like(side)
        edge = (
            side
            + jnp.where(has_top, lon_pick(down_edge, spot, 1), zero)
            + jnp.where(has_bottom, lon_pick(up_edge, spot, -1), zero)
        )
    from_top = jnp.where(has_top, from_top, jnp.zeros_like(from_top))
    from_bottom = jnp.where(has_bottom, from_bottom, jnp.zeros_like(from_bottom))
    own = jnp.concatenate([from_top[:REACH], state, from_bottom[:REACH], edge[:1]], axis=0)
    base_edge = jnp.concatenate([from_top[REACH:], from_bottom[REACH:], edge[1:]], axis=0)

    lift, conv_a, conv_b, out_lanes = lane_weights(lift_weight, conv_weights, out_weight)
    tm_count = lax.axis_size("tm")

    def neighbours(array):
        return (
            lax.ppermute(array, "tm", ring_perm(tm_count, 1)),
            lax.ppermute(array, "tm", ring_perm(tm_count, -1)),
        )

    geometry = (frames, chans, rows, ring, pad, chunk)

    def scratch(in_rows):
        return [
            pltpu.VMEM((3, frames, in_rows, pad, LANES), BF),
            pltpu.VMEM((3, frames, in_rows - 2, pad, LANES), BF),
            pltpu.VMEM((chunk * pad, 2 * LANES), F32),
            pltpu.VMEM((LANES, 2 * LANES), F32),
        ]

    prev, following = neighbours(own)
    nxt, current = pl.pallas_call(
        functools.partial(first_kernel, geometry),
        out_shape=(shape((rows + 5, fc, cols), BF), shape((rows + 4, fc, cols), F32)),
        in_specs=[smem] + [vmem] * 9,
        out_specs=[vmem] * 2,
        scratch_shapes=scratch(rows + 2 * REACH) + [pltpu.VMEM((frames, LANES, LANES), F32)],
        compiler_params=pltpu.CompilerParams(vmem_limit_bytes=GRANT),
    )(step_sizes, own, prev, following, base, base_edge, lift, conv_a, conv_b, out_lanes)

    prev, following = neighbours(nxt)
    result = pl.pallas_call(
        functools.partial(last_kernel, geometry),
        out_shape=shape((fc * rows, cols), F32),
        in_specs=[smem] + [vmem] * 11,
        out_specs=vmem,
        scratch_shapes=scratch(rows + 4),
        compiler_params=pltpu.CompilerParams(vmem_limit_bytes=GRANT),
    )(
        step_sizes, nxt, prev, following, current, flat(observed), flat(obs_weight),
        noise_field.reshape(-1, cols), lift, conv_a, conv_b, out_lanes,
    )
    return result.reshape(prior_state.shape)


def solution(mesh):
    placed = (
        P(("groups", "tm"), None, "lat", "lon"),
        P(("groups", "tm"), None, "lat", "lon"),
        P(("groups", "tm"), None, "lat", "lon"),
        P(None, ("groups", "tm"), None, "lat", "lon"),
        P(),
        P(),
        P(),
        P(),
    )
    return jax.shard_map(
        per_device,
        mesh=mesh,
        in_specs=placed,
        out_specs=P(("groups", "tm"), None, "lat", "lon"),
        check_vma=False,
    )
```

```python
import functools

import jax
import jax.numpy as jnp
from jax import lax
from jax.experimental import pallas as pl
from jax.experimental.pallas import tpu as pltpu
from jax.sharding import PartitionSpec as P

LANES = 128
REACH = 4
EDGE = 2 * REACH
GUARD = 8
SLABS = 8
SUMS = 4
AHEAD = 2
LIFT_ROWS = 2
CHUNK = 7
GRANT = 24 << 20
BF = jnp.bfloat16
F32 = jnp.float32


def ring_edges(rows_of, rows, first, count, lanes):
    lane = lax.broadcasted_iota(jnp.int32, rows_of(0).shape, 1)
    tile = jnp.zeros(rows_of(0).shape, F32)
    for row in range(count):
        at = first + EDGE * row
        value = rows_of(rows + row)
        low = pltpu.roll(value, at % lanes, 1)
        high = pltpu.roll(value, (at + EDGE) % lanes, 1)
        tile = jnp.where((lane >= at) & (lane < at + REACH), low, tile)
        tile = jnp.where((lane >= at + REACH) & (lane < at + EDGE), high, tile)
    return tile


def pack_kernel(
    geometry, step_in, prior_in, observed_in, weight_in, noise_in,
    state_out, base_out, lon_out, *rest,
):
    frames, chans, rows, single = geometry
    *outs, state, base, prior, observed, weight, noise, step_ref, done = rest
    size = frames * chans * rows
    copies = [
        pltpu.make_async_copy(source.at[:size], target, done.at[index])
        for index, (source, target) in enumerate(
            ((prior_in, prior), (observed_in, observed), (weight_in, weight), (noise_in, noise))
        )
    ] + [pltpu.make_async_copy(step_in, step_ref, done.at[4])]
    for copy in copies:
        copy.start()
    for copy in copies:
        copy.wait()
    step = step_ref[0]
    spread = jnp.sqrt(jnp.full((chans, LANES), 2.0 * step, F32))
    for row in range(rows):
        for frame in range(frames):
            part = pl.ds(frame * chans * rows + row, chans, stride=rows)
            own = prior[part, :]
            state[row, frame * chans : (frame + 1) * chans, :] = own
            base[row, frame * chans : (frame + 1) * chans, :] = (
                own + step * (weight[part, :] * (observed[part, :] - own)) + spread * noise[part, :]
            )
    for row in range(rows):
        state_out[row] = state[row].astype(BF)
        base_out[row] = base[row]
    lon_out[0] = ring_edges(lambda r: state[r], 0, EDGE * REACH, rows, LANES).astype(BF)
    lon_out[1] = ring_edges(lambda r: base[r], 0, EDGE * 2, rows, LANES).astype(BF)
    sides = []
    for start, at in ((rows - REACH, 0), (0, rows + REACH)):
        skip = start + 2 if at == 0 else start
        at_base = 0 if at == 0 else rows + 2
        tiles = [state[start + row] for row in range(REACH)] + [base[skip + row] for row in range(2)]
        tiles.append(ring_edges(lambda r: state[r], start, EDGE * at, REACH, LANES))
        tiles.append(ring_edges(lambda r: base[r], skip, EDGE * at_base, 2, LANES))
        sides.append(tiles)
    if single:
        upward = lax.axis_index("lat") > 0
        sides = [[jnp.where(upward, up, down) for down, up in zip(*sides)]]
    for tiles, rows_out, edge_out in zip(sides, outs[::2], outs[1::2]):
        for place, tile in enumerate(tiles[: REACH + 2]):
            rows_out[place] = tile.astype(BF)
        for place, tile in enumerate(tiles[REACH + 2 :]):
            edge_out[place] = tile.astype(BF)


def features(geometry, in_rows, own, prev, following, lift, act, slabs, turned, lifted):
    frames, ring = geometry
    for tile in range(in_rows + 1):
        stacked = jnp.concatenate([prev[tile], own[tile], following[tile]] * 2, axis=0)
        turned[tile * LANES : (tile + 1) * LANES, :] = jnp.transpose(stacked.astype(F32)).astype(BF)
    halo = in_rows * LANES
    lifted[...] = jnp.dot(turned[halo:, :], lift[...], preferred_element_type=F32)
    for first in range(0, in_rows, LIFT_ROWS):
        count = min(LIFT_ROWS, in_rows - first)
        low = first * LANES
        block = jnp.dot(
            turned[low : low + count * LANES, :], lift[...], preferred_element_type=F32
        )
        for row in range(first, first + count):
            for frame in range(frames):
                part = slice(frame * LANES, (frame + 1) * LANES)
                start = (row - first) * LANES
                value = jnp.concatenate(
                    [block[start : start + LANES, part], lifted[row * EDGE : (row + 1) * EDGE, part]],
                    axis=0,
                )
                store_shifts(act, slabs[(2 * row + frame) % SLABS], frame, row, ring, value)


def store_shifts(act, slab, frame, row, ring, value):
    at = GUARD
    slab[at : at + ring, :] = value
    slab[at - 1 : at, :] = value[ring - 1 :]
    slab[at + ring : at + ring + 1, :] = value[:1]
    act[0, frame, row, :ring, :] = slab[at - 1 : at - 1 + ring, :].astype(BF)
    act[1, frame, row, :ring, :] = value.astype(BF)
    act[2, frame, row, :ring, :] = slab[at + 1 : at + 1 + ring, :].astype(BF)


def conv_pairs(act, frame, weight, first, count):
    pieces = [
        jnp.concatenate([act[col, frame, 2 * (first + p) + row] for p in range(count)], axis=0)
        for row in range(4)
        for col in range(3)
    ]
    return jnp.dot(jnp.concatenate(pieces, axis=1), weight[...], preferred_element_type=F32)


def gated(half):
    return half + half * jnp.tanh(half)


def convolve(
    geometry, in_rows, reach, act, act2, slabs, sums, conv_a, conv_b, top, bottom, emit
):
    frames, ring, pad, chunk = geometry
    waiting = []

    def finish():
        into, frame, first, count, place = waiting.pop(0)
        for p in range(count):
            for q in range(2):
                row = 2 * (first + p) + q
                value = gated(into[p * pad : p * pad + ring, q * LANES : (q + 1) * LANES])
                if place == 2:
                    merged = act[1, frame, row + 2, :ring, :].astype(F32) + value
                    emit(frame, row, merged)
                    continue
                if row + 1 < reach:
                    value = value * top
                if row + 1 >= in_rows - reach:
                    value = value * bottom
                store_shifts(act2, slabs[row % SLABS], frame, row, ring, value)

    used = 0
    for place, source, weight in ((1, act, conv_a), (2, act2, conv_b)):
        pairs = (in_rows - 2 * place) // 2
        for frame in range(frames):
            for first in range(0, pairs, chunk):
                count = min(chunk, pairs - first)
                while any(w[4] < place and w[1] == frame for w in waiting):
                    finish()
                into = sums[used % len(sums)]
                used += 1
                into[: count * pad, :] = conv_pairs(source, frame, weight, first, count)
                waiting.append((into, frame, first, count, place))
                if len(waiting) > AHEAD:
                    finish()
    while waiting:
        finish()


def edge_flags():
    lat = lax.axis_index("lat")
    top = jnp.where(lat > 0, 1.0, 0.0).astype(F32)
    bottom = jnp.where(lat < lax.axis_size("lat") - 1, 1.0, 0.0).astype(F32)
    return top, bottom


def project(out_weight, merged):
    return lax.dot_general(
        out_weight[...], merged, (((1,), (1,)), ((), ())), preferred_element_type=F32
    )


def first_kernel(
    geometry, step_ref, own, prev, following, base, base_edge, lift, conv_a, conv_b, out_weight,
    next_out, state_out, act, act2, turned, lifted, halo_merged, *rest,
):
    slabs, sums = rest[:SLABS], rest[SLABS:]
    frames, chans, rows, ring, pad, chunk = geometry
    in_rows, out_rows = rows + 2 * REACH, rows + 4
    top, bottom = edge_flags()
    step = step_ref[0]
    features((frames, ring), in_rows, own, prev, following, lift, act, slabs, turned, lifted)

    def emit(frame, row, merged):
        score = project(out_weight, merged[:LANES].astype(BF))
        part = slice(frame * chans, (frame + 1) * chans)
        if row < 2:
            start = base_edge[row, part, :].astype(F32)
        elif row < rows + 2:
            start = base[row - 2, part, :]
        else:
            start = base_edge[row - rows, part, :].astype(F32)
        value = start + step * score
        if row < 2:
            value = value * top
        if row >= rows + 2:
            value = value * bottom
        state_out[row, part, :] = value
        halo_merged[frame, row * EDGE : (row + 1) * EDGE, :] = merged[LANES:]

    convolve(
        (frames, ring, pad, chunk), in_rows, REACH, act, act2, slabs, sums, conv_a, conv_b,
        top, bottom, emit,
    )
    for row in range(out_rows):
        next_out[row] = state_out[row].astype(BF)
    edges = [project(out_weight, halo_merged[frame].astype(BF)) for frame in range(frames)]
    score = jnp.concatenate(edges, axis=0)
    value = base_edge[4].astype(F32) + step * score
    lane = lax.broadcasted_iota(jnp.int32, value.shape, 1)
    value = jnp.where(lane < 2 * EDGE, value * top, value)
    value = jnp.where(lane >= (rows + 2) * EDGE, value * bottom, value)
    value = jnp.where(lane < out_rows * EDGE, value, 0.0)
    next_out[out_rows] = value.astype(BF)


def last_kernel(
    geometry, step_ref, own, prev, following, state, observed, weight, noise, lift, conv_a, conv_b,
    out_weight, result, act, act2, turned, lifted, *rest,
):
    slabs, sums = rest[:SLABS], rest[SLABS:]
    frames, chans, rows, ring, pad, chunk = geometry
    in_rows = rows + 4
    top, bottom = edge_flags()
    step = step_ref[1]
    spread = jnp.sqrt(jnp.full((chans, LANES), 2.0 * step, F32))
    features((frames, ring), in_rows, own, prev, following, lift, act, slabs, turned, lifted)

    def emit(frame, row, merged):
        score = project(out_weight, merged[:LANES].astype(BF))
        part = pl.ds(frame * chans * rows + row, chans, stride=rows)
        late = pl.ds((frames + frame) * chans * rows + row, chans, stride=rows)
        before = state[row + 2, frame * chans : (frame + 1) * chans, :]
        result[part, :] = (
            before
            + step * (score + weight[part, :] * (observed[part, :] - before))
            + spread * noise[late, :]
        )

    convolve(
        (frames, ring, pad, chunk), in_rows, 2, act, act2, slabs, sums, conv_a, conv_b, top, bottom,
        emit,
    )


def ring_perm(count, by):
    return [(i, (i + by) % count) for i in range(count)]


def lane_weights(lift_weight, conv_weights, out_weight):
    hidden, stacked = lift_weight.shape
    gap = LANES - hidden
    chans = out_weight.shape[0]
    turned = lift_weight.T
    lanes = [
        jnp.pad(turned, ((frame * chans, (1 - frame) * chans), (0, gap))) for frame in range(2)
    ]
    lift = jnp.concatenate(lanes, axis=1)
    block = 2 * chans
    tm = lax.axis_index("tm")
    kept = jnp.concatenate(
        [
            jnp.full((block, 1), jnp.where(tm > 0, 1.0, 0.0), F32),
            jnp.ones((block, 1), F32),
            jnp.full((block, 1), jnp.where(tm < lax.axis_size("tm") - 1, 1.0, 0.0), F32),
        ],
        axis=0,
    )
    lift = lift * kept
    high = lax.reduce_precision(lift, 8, 7)
    lift = jnp.concatenate([high, lift - high], axis=0).astype(BF)
    half = conv_weights * jnp.asarray(0.5, BF)
    taps = jnp.swapaxes(half, 2, 3).reshape(2, 3, 3, hidden, hidden)
    taps = jnp.pad(taps, ((0, 0), (0, 0), (0, 0), (0, gap), (0, gap)))
    pair = jnp.concatenate(
        [
            jnp.pad(taps, ((0, 0), (0, 1), (0, 0), (0, 0), (0, 0))),
            jnp.pad(taps, ((0, 0), (1, 0), (0, 0), (0, 0), (0, 0))),
        ],
        axis=4,
    )
    conv = pair.reshape(2, 12 * LANES, 2 * LANES)
    return lift, conv[0], conv[1], jnp.pad(out_weight, ((0, 0), (0, gap)))


def per_device(
    prior_state, observed, obs_weight, noise_field, step_sizes, lift_weight, conv_weights, out_weight
):
    frames, chans, rows, cols = prior_state.shape
    lat_count, lon_count = lax.axis_size("lat"), lax.axis_size("lon")
    fc = frames * chans
    ring, pad, chunk = cols + EDGE, cols + 16, CHUNK
    smem = pl.BlockSpec(memory_space=pltpu.SMEM)
    vmem = pl.BlockSpec(memory_space=pltpu.VMEM)
    shape = jax.ShapeDtypeStruct
    flat = lambda array: array.reshape(fc * rows, cols)

    sides = (shape((REACH + 2, fc, cols), BF), shape((2, fc, cols), BF)) * (
        1 if lat_count == 2 else 2
    )
    state, base, lon_edge, *outward = pl.pallas_call(
        functools.partial(pack_kernel, (frames, chans, rows, lat_count == 2)),
        out_shape=(
            shape((rows, fc, cols), BF),
            shape((rows, fc, cols), F32),
            shape((2, fc, cols), BF),
            *sides,
        ),
        in_specs=[pl.BlockSpec(memory_space=pltpu.HBM)] * 5,
        out_specs=[vmem] * (3 + len(sides)),
        scratch_shapes=[
            *[pltpu.VMEM((rows, fc, cols), F32)] * 2,
            *[pltpu.VMEM((fc * rows, cols), F32)] * 4,
            pltpu.SMEM(step_sizes.shape, F32),
            pltpu.SemaphoreType.DMA((5,)),
        ],
        compiler_params=pltpu.CompilerParams(vmem_limit_bytes=GRANT),
    )(
        *[
            pltpu.with_memory_space_constraint(array, pltpu.HBM)
            for array in (
                step_sizes, flat(prior_state), flat(observed), flat(obs_weight), noise_field.reshape(-1, cols)
            )
        ],
    )

    lat = lax.axis_index("lat")
    spot = ("lat", "lon")

    def lon_pick(array, axes, lat_shift):
        def move(by):
            perm = []
            for a in range(lat_count):
                for o in range(lon_count):
                    b = (a + lat_shift) % lat_count
                    perm.append((a * lon_count + o, b * lon_count + (o + by) % lon_count))
            return lax.ppermute(array, spot, perm)

        if lon_count <= 2:
            return move(lon_count - 1)
        lane = lax.broadcasted_iota(jnp.int32, array.shape, array.ndim - 1)
        return jnp.where(lane % EDGE < REACH, move(-1), move(1))

    has_top, has_bottom = lat > 0, lat < lat_count - 1
    side = lon_pick(lon_edge, spot, 0)
    if lat_count == 2:
        rows_in = lax.ppermute(outward[0], "lat", ring_perm(2, 1))
        corner = lon_pick(outward[1], spot, 1)
        from_top, from_bottom = rows_in, rows_in
        edge = side + corner
    else:
        down_rows, down_edge, up_rows, up_edge = outward
        from_top = lax.ppermute(down_rows, "lat", ring_perm(lat_count, 1))
        from_bottom = lax.ppermute(up_rows, "lat", ring_perm(lat_count, -1))
        zero = jnp.zeros_like(side)
        edge = (
            side
            + jnp.where(has_top, lon_pick(down_edge, spot, 1), zero)
            + jnp.where(has_bottom, lon_pick(up_edge, spot, -1), zero)
        )
    from_top = jnp.where(has_top, from_top, jnp.zeros_like(from_top))
    from_bottom = jnp.where(has_bottom, from_bottom, jnp.zeros_like(from_bottom))
    own = jnp.concatenate([from_top[:REACH], state, from_bottom[:REACH], edge[:1]], axis=0)
    base_edge = jnp.concatenate([from_top[REACH:], from_bottom[REACH:], edge[1:]], axis=0)

    conv_weights, own = lax.optimization_barrier((conv_weights, own))
    lift, conv_a, conv_b, out_lanes = lane_weights(lift_weight, conv_weights, out_weight)
    tm_count = lax.axis_size("tm")

    def neighbours(array):
        return (
            lax.ppermute(array, "tm", ring_perm(tm_count, 1)),
            lax.ppermute(array, "tm", ring_perm(tm_count, -1)),
        )

    geometry = (frames, chans, rows, ring, pad, chunk)

    def scratch(in_rows, *more):
        return [
            pltpu.VMEM((3, frames, in_rows, pad, LANES), BF),
            pltpu.VMEM((3, frames, in_rows - 2, pad, LANES), BF),
            pltpu.VMEM(((in_rows + 1) * LANES, 6 * fc), BF),
            pltpu.VMEM((LANES, 2 * LANES), F32),
            *more,
            *[pltpu.VMEM((ring + 2 * GUARD, LANES), F32)] * SLABS,
            *[pltpu.VMEM((chunk * pad, 2 * LANES), F32)] * SUMS,
        ]

    prev, following = neighbours(own)
    nxt, current = pl.pallas_call(
        functools.partial(first_kernel, geometry),
        out_shape=(shape((rows + 5, fc, cols), BF), shape((rows + 4, fc, cols), F32)),
        in_specs=[smem] + [vmem] * 9,
        out_specs=[vmem] * 2,
        scratch_shapes=scratch(rows + 2 * REACH, pltpu.VMEM((frames, LANES, LANES), F32)),
        compiler_params=pltpu.CompilerParams(vmem_limit_bytes=GRANT),
    )(step_sizes, own, prev, following, base, base_edge, lift, conv_a, conv_b, out_lanes)

    prev, following = neighbours(nxt)
    result = pl.pallas_call(
        functools.partial(last_kernel, geometry),
        out_shape=shape((fc * rows, cols), F32),
        in_specs=[smem] + [vmem] * 11,
        out_specs=vmem,
        scratch_shapes=scratch(rows + 4),
        compiler_params=pltpu.CompilerParams(vmem_limit_bytes=GRANT),
    )(
        step_sizes, nxt, prev, following, current, flat(observed), flat(obs_weight),
        noise_field.reshape(-1, cols), lift, conv_a, conv_b, out_lanes,
    )
    return result.reshape(prior_state.shape)


def solution(mesh):
    placed = (
        P(("groups", "tm"), None, "lat", "lon"),
        P(("groups", "tm"), None, "lat", "lon"),
        P(("groups", "tm"), None, "lat", "lon"),
        P(None, ("groups", "tm"), None, "lat", "lon"),
        P(),
        P(),
        P(),
        P(),
    )
    return jax.shard_map(
        per_device,
        mesh=mesh,
        in_specs=placed,
        out_specs=P(("groups", "tm"), None, "lat", "lon"),
        check_vma=False,
    )
```

```python
import functools

import jax
import jax.numpy as jnp
from jax import lax
from jax.experimental import pallas as pl
from jax.experimental.pallas import tpu as pltpu
from jax.sharding import PartitionSpec as P


LANES = 128
REACH = 4
EDGE = 2 * REACH
GUARD = 8
SLABS = 16
AHEAD = 3
PARTS = 2
LIFT_PAIRS = 4
GRANT = 24 << 20
BF = jnp.bfloat16
F32 = jnp.float32


def ring_edges(rows_of, rows, first, count, lanes):
    lane = lax.broadcasted_iota(jnp.int32, rows_of(0).shape, 1)
    tile = jnp.zeros(rows_of(0).shape, F32)
    for row in range(count):
        at = first + EDGE * row
        value = rows_of(rows + row)
        low = pltpu.roll(value, at % lanes, 1)
        high = pltpu.roll(value, (at + EDGE) % lanes, 1)
        tile = jnp.where((lane >= at) & (lane < at + REACH), low, tile)
        tile = jnp.where((lane >= at + REACH) & (lane < at + EDGE), high, tile)
    return tile


def pack_kernel(
    geometry, step_in, prior_in, observed_in, weight_in, noise_in,
    state_out, base_out, lon_out, *rest,
):
    frames, chans, rows, single = geometry
    *outs, state, base, prior, observed, weight, noise, step_ref, done = rest
    size = frames * chans * rows
    copies = [
        pltpu.make_async_copy(source.at[:size], target, done.at[index])
        for index, (source, target) in enumerate(
            ((prior_in, prior), (observed_in, observed), (weight_in, weight), (noise_in, noise))
        )
    ] + [pltpu.make_async_copy(step_in, step_ref, done.at[4])]
    for copy in copies:
        copy.start()
    for copy in copies:
        copy.wait()
    step = step_ref[0]
    spread = jnp.sqrt(jnp.full((chans, LANES), 2.0 * step, F32))
    for row in range(rows):
        for frame in range(frames):
            part = pl.ds(frame * chans * rows + row, chans, stride=rows)
            own = prior[part, :]
            state[row, frame * chans : (frame + 1) * chans, :] = own
            base[row, frame * chans : (frame + 1) * chans, :] = (
                own + step * (weight[part, :] * (observed[part, :] - own)) + spread * noise[part, :]
            )
    for row in range(rows):
        state_out[row] = state[row].astype(BF)
        base_out[row] = base[row]
    lon_out[0] = ring_edges(lambda r: state[r], 0, EDGE * REACH, rows, LANES).astype(BF)
    lon_out[1] = ring_edges(lambda r: base[r], 0, EDGE * 2, rows, LANES).astype(BF)
    sides = []
    for start, at in ((rows - REACH, 0), (0, rows + REACH)):
        skip = start + 2 if at == 0 else start
        at_base = 0 if at == 0 else rows + 2
        tiles = [state[start + row] for row in range(REACH)] + [base[skip + row] for row in range(2)]
        tiles.append(ring_edges(lambda r: state[r], start, EDGE * at, REACH, LANES))
        tiles.append(ring_edges(lambda r: base[r], skip, EDGE * at_base, 2, LANES))
        sides.append(tiles)
    if single:
        upward = lax.axis_index("lat") > 0
        sides = [[jnp.where(upward, up, down) for down, up in zip(*sides)]]
    for tiles, rows_out, edge_out in zip(sides, outs[::2], outs[1::2]):
        for place, tile in enumerate(tiles[: REACH + 2]):
            rows_out[place] = tile.astype(BF)
        for place, tile in enumerate(tiles[REACH + 2 :]):
            edge_out[place] = tile.astype(BF)


def place_of(tile, in_rows):
    return tile if tile == in_rows else (tile % 2) * (in_rows // 2) + tile // 2


def features(geometry, in_rows, own, prev, following, lift, slabs, turned, lifted):
    frames, ring = geometry
    half = in_rows // 2
    for tile in range(in_rows + 1):
        stacked = jnp.concatenate([prev[tile], own[tile], following[tile]] * 2, axis=0)
        at = place_of(tile, in_rows) * LANES
        turned[at : at + LANES, :] = jnp.transpose(stacked.astype(F32)).astype(BF)
    for parity in range(2):
        lifted[parity] = jnp.dot(
            turned[in_rows * LANES :, :], lift[parity], preferred_element_type=F32
        )
    for first in range(0, half, LIFT_PAIRS):
        count = min(LIFT_PAIRS, half - first)
        for parity in range(2):
            low = (parity * half + first) * LANES
            block = jnp.dot(
                turned[low : low + count * LANES, :], lift[parity], preferred_element_type=F32
            )
            for place in range(count):
                row = 2 * (first + place) + parity
                for frame in range(frames):
                    part = slice(frame * LANES, (frame + 1) * LANES)
                    main = block[place * LANES : (place + 1) * LANES, part]
                    edge = lifted[parity, row * EDGE : (row + 1) * EDGE, part]
                    fill_slab(slabs.at[frame, row], ring, jnp.concatenate([main, edge], axis=0))


def fill_slab(slab, ring, value):
    at = GUARD
    slab[at : at + ring, :] = value
    slab[at - 1 : at, :] = value[ring - 1 :]
    slab[at + ring : at + ring + 1, :] = value[:1]


def store_pair(act, slabs, frame, pair, ring):
    at = GUARD
    even, odd = [slab[at : at + ring, :] for slab in slabs]
    left_even, left_odd = [slab[at - 1 : at - 1 + ring, :] for slab in slabs]
    right_even, right_odd = [slab[at + 1 : at + 1 + ring, :] for slab in slabs]
    lane = lax.broadcasted_iota(jnp.int32, even.shape, 1)
    quarter, half, most = LANES // 4, LANES // 2, 3 * LANES // 4
    blocks = (
        jnp.where(lane < most, left_even, even),
        jnp.where(lane < quarter, right_even, even),
        jnp.where((lane < quarter) | (lane >= half), left_odd, odd),
        jnp.where((lane >= half) & (lane < most), right_odd, odd),
        jnp.where((lane >= quarter) & (lane < most), right_even, right_odd),
    )
    for index, block in enumerate(blocks):
        act[frame, pair, :ring, index * LANES : (index + 1) * LANES] = block.astype(BF)


def arranged(weight, parity):
    hidden = weight.shape[0]
    quarter = LANES - hidden
    if parity == 0:
        return jnp.concatenate([weight, weight[:quarter]], axis=0)
    return jnp.concatenate(
        [weight[2 * quarter :], weight[:quarter], weight[: 2 * quarter]], axis=0
    )


def tap_kernel(conv_in, conv_a, conv_b):
    hidden = conv_in.shape[-1]
    quarter = LANES - hidden
    for index, out in enumerate((conv_a, conv_b)):
        out[...] = jnp.zeros(out.shape, BF)
        for down in range(3):
            for side in range(3):
                tap = conv_in[index, 3 * down + side].astype(F32) * 0.5
                for q in range(2):
                    row = down + q
                    block, odd = divmod(row, 2)
                    base = 5 * LANES * block + 2 * LANES * odd
                    turned = jnp.transpose(arranged(tap, q)).astype(BF)
                    if side == 0:
                        spans = [(0, 0, hidden)]
                    elif side == 1:
                        spans = [(hidden, 0, quarter), (LANES + quarter, quarter, hidden)]
                    else:
                        spans = [(LANES, 0, quarter)]
                    lanes = slice(q * LANES, (q + 1) * LANES)
                    for at, low, high in spans:
                        for step in range(low, high, quarter):
                            vreg, lane = divmod(at + step - low, LANES)
                            lane = (lane + odd * LANES // 2) % LANES
                            where = base + vreg * LANES + lane
                            out[where : where + quarter, lanes] = turned[step : step + quarter]
                    if side == 2:
                        for step in range(quarter, hidden, quarter):
                            lane = (step + odd * LANES // 2) % LANES
                            where = 5 * LANES * block + 4 * LANES + lane
                            out[where : where + quarter, lanes] = turned[step : step + quarter]


def conv_pairs(act, frame, weight, first, count):
    rows = [
        jnp.concatenate([act[frame, first + p], act[frame, first + p + 1]], axis=1)
        for p in range(count)
    ]
    return jnp.dot(jnp.concatenate(rows, axis=0), weight[...], preferred_element_type=F32)


def gated(half):
    return half + half * jnp.tanh(half)


def convolve(
    geometry, in_rows, reach, slabs, spare, act, act2, conv_a, conv_b, top, bottom, emit
):
    frames, ring, pad = geometry
    waiting = []

    def finish():
        sums, frame, first, count, place = waiting.pop(0)
        for p in range(count):
            pair = first + p
            for q in range(2):
                row = 2 * pair + q
                value = gated(sums[p * pad : p * pad + ring, q * LANES : (q + 1) * LANES])
                if place == 2:
                    own = slabs[frame, row + 2, GUARD : GUARD + ring, :].astype(BF)
                    emit(frame, row, own.astype(F32) + value)
                    continue
                if row + 1 < reach:
                    value = value * top
                if row + 1 >= in_rows - reach:
                    value = value * bottom
                fill_slab(spare[row % SLABS], ring, value)
            if place == 1:
                at = 2 * pair % SLABS
                store_pair(act2, spare[at : at + 2], frame, pair, ring)

    for place, source, weight in ((1, act, conv_a), (2, act2, conv_b)):
        pairs = (in_rows - 2 * place) // 2
        chunk = -(-pairs // PARTS)
        for frame in range(frames):
            if place == 1:
                for pair in range(in_rows // 2):
                    at = 2 * pair
                    store_pair(act, [slabs.at[frame, at], slabs.at[frame, at + 1]], frame, pair, ring)
            for first in range(0, pairs, chunk):
                count = min(chunk, pairs - first)
                while any(w[4] < place and w[1] == frame for w in waiting):
                    finish()
                sums = conv_pairs(source, frame, weight, first, count)
                waiting.append((sums, frame, first, count, place))
                if len(waiting) > AHEAD:
                    finish()
    while waiting:
        finish()


def edge_flags():
    lat = lax.axis_index("lat")
    top = jnp.where(lat > 0, 1.0, 0.0).astype(F32)
    bottom = jnp.where(lat < lax.axis_size("lat") - 1, 1.0, 0.0).astype(F32)
    return top, bottom


def project(out_weight, merged):
    return lax.dot_general(
        out_weight, merged, (((1,), (1,)), ((), ())), preferred_element_type=F32
    )


def first_kernel(
    geometry, step_in, own, prev, following, base, base_edge, lift, conv_a, conv_b, out_weight,
    next_out, state_out, act, act2, slabs, turned, lifted, halo_merged, step_ref, done, *spare,
):
    frames, chans, rows, ring, pad = geometry
    in_rows, out_rows = rows + 2 * REACH, rows + 4
    steps = pltpu.make_async_copy(step_in, step_ref, done)
    steps.start()
    top, bottom = edge_flags()
    features((frames, ring), in_rows, own, prev, following, lift, slabs, turned, lifted)
    steps.wait()
    step = step_ref[0]

    def emit(frame, row, merged):
        score = project(out_weight[row % 2], merged[:LANES].astype(BF))
        part = slice(frame * chans, (frame + 1) * chans)
        if row < 2:
            start = base_edge[row, part, :].astype(F32)
        elif row < rows + 2:
            start = base[row - 2, part, :]
        else:
            start = base_edge[row - rows, part, :].astype(F32)
        value = start + step * score
        if row < 2:
            value = value * top
        if row >= rows + 2:
            value = value * bottom
        state_out[row, part, :] = value
        halo_merged[row % 2, frame, row * EDGE : (row + 1) * EDGE, :] = merged[LANES:]

    convolve(
        (frames, ring, pad), in_rows, REACH, slabs, spare, act, act2, conv_a, conv_b,
        top, bottom, emit,
    )
    for row in range(out_rows):
        next_out[row] = state_out[row].astype(BF)
    even, odd = [
        jnp.concatenate(
            [
                project(out_weight[parity], halo_merged[parity, frame].astype(BF))
                for frame in range(frames)
            ],
            axis=0,
        )
        for parity in range(2)
    ]
    lane = lax.broadcasted_iota(jnp.int32, even.shape, 1)
    score = jnp.where((lane // EDGE) % 2 == 0, even, odd)
    value = base_edge[4].astype(F32) + step * score
    value = jnp.where(lane < 2 * EDGE, value * top, value)
    value = jnp.where(lane >= (rows + 2) * EDGE, value * bottom, value)
    value = jnp.where(lane < out_rows * EDGE, value, 0.0)
    next_out[out_rows] = value.astype(BF)


def last_kernel(
    geometry, step_in, own, prev, following, state, observed, weight, noise, lift, conv_a, conv_b,
    out_weight, result, act, act2, slabs, turned, lifted, step_ref, done, *spare,
):
    frames, chans, rows, ring, pad = geometry
    in_rows = rows + 4
    steps = pltpu.make_async_copy(step_in, step_ref, done)
    steps.start()
    top, bottom = edge_flags()
    features((frames, ring), in_rows, own, prev, following, lift, slabs, turned, lifted)
    steps.wait()
    step = step_ref[1]
    spread = jnp.sqrt(jnp.full((chans, LANES), 2.0 * step, F32))

    def emit(frame, row, merged):
        score = project(out_weight[row % 2], merged[:LANES].astype(BF))
        part = pl.ds(frame * chans * rows + row, chans, stride=rows)
        late = pl.ds((frames + frame) * chans * rows + row, chans, stride=rows)
        before = state[row + 2, frame * chans : (frame + 1) * chans, :]
        result[part, :] = (
            before
            + step * (score + weight[part, :] * (observed[part, :] - before))
            + spread * noise[late, :]
        )

    convolve(
        (frames, ring, pad), in_rows, 2, slabs, spare, act, act2, conv_a, conv_b, top, bottom,
        emit,
    )


def ring_perm(count, by):
    return [(i, (i + by) % count) for i in range(count)]


def lane_weights(lift_weight, out_weight):
    hidden, _ = lift_weight.shape
    gap = LANES - hidden
    chans = out_weight.shape[0]
    block = 2 * chans
    tm = lax.axis_index("tm")
    kept = jnp.concatenate(
        [
            jnp.full((block, 1), jnp.where(tm > 0, 1.0, 0.0), F32),
            jnp.ones((block, 1), F32),
            jnp.full((block, 1), jnp.where(tm < lax.axis_size("tm") - 1, 1.0, 0.0), F32),
        ],
        axis=0,
    )
    lifts = []
    for parity in range(2):
        turned = arranged(lift_weight, parity).T
        lanes = [jnp.pad(turned, ((frame * chans, (1 - frame) * chans), (0, 0))) for frame in range(2)]
        lift = jnp.concatenate(lanes, axis=1) * kept
        high = lax.reduce_precision(lift, 8, 7)
        lifts.append(jnp.concatenate([high, lift - high], axis=0).astype(BF))
    even = jnp.pad(out_weight, ((0, 0), (0, gap)))
    return jnp.stack(lifts), jnp.stack([even, jnp.roll(even, LANES // 2, axis=1)])


def per_device(
    prior_state, observed, obs_weight, noise_field, step_sizes, lift_weight, conv_weights, out_weight
):
    frames, chans, rows, cols = prior_state.shape
    lat_count, lon_count = lax.axis_size("lat"), lax.axis_size("lon")
    fc = frames * chans
    assert cols == LANES and (rows + EDGE) * EDGE == LANES and fc == 16 and frames == 2
    assert 4 * lift_weight.shape[0] == 3 * LANES and noise_field.shape[0] == 2
    ring, pad = cols + EDGE, cols + 16
    hbm = pl.BlockSpec(memory_space=pltpu.HBM)
    steps = pltpu.with_memory_space_constraint(step_sizes, pltpu.HBM)
    vmem = pl.BlockSpec(memory_space=pltpu.VMEM)
    shape = jax.ShapeDtypeStruct
    flat = lambda array: array.reshape(fc * rows, cols)

    sides = (shape((REACH + 2, fc, cols), BF), shape((2, fc, cols), BF)) * (
        1 if lat_count == 2 else 2
    )
    state, base, lon_edge, *outward = pl.pallas_call(
        functools.partial(pack_kernel, (frames, chans, rows, lat_count == 2)),
        out_shape=(
            shape((rows, fc, cols), BF),
            shape((rows, fc, cols), F32),
            shape((2, fc, cols), BF),
            *sides,
        ),
        in_specs=[hbm] * 5,
        out_specs=[vmem] * (3 + len(sides)),
        scratch_shapes=[
            *[pltpu.VMEM((rows, fc, cols), F32)] * 2,
            *[pltpu.VMEM((fc * rows, cols), F32)] * 4,
            pltpu.SMEM(step_sizes.shape, F32),
            pltpu.SemaphoreType.DMA((5,)),
        ],
        compiler_params=pltpu.CompilerParams(vmem_limit_bytes=GRANT),
    )(
        *[
            pltpu.with_memory_space_constraint(array, pltpu.HBM)
            for array in (
                step_sizes, flat(prior_state), flat(observed), flat(obs_weight), noise_field.reshape(-1, cols)
            )
        ],
    )

    lat = lax.axis_index("lat")
    spot = ("lat", "lon")

    def lon_pick(array, lat_shift):
        def move(by):
            perm = []
            for a in range(lat_count):
                for o in range(lon_count):
                    b = (a + lat_shift) % lat_count
                    perm.append((a * lon_count + o, b * lon_count + (o + by) % lon_count))
            return lax.ppermute(array, spot, perm)

        if lon_count <= 2:
            return move(lon_count - 1)
        lane = lax.broadcasted_iota(jnp.int32, array.shape, array.ndim - 1)
        return jnp.where(lane % EDGE < REACH, move(-1), move(1))

    has_top, has_bottom = lat > 0, lat < lat_count - 1
    side = lon_pick(lon_edge, 0)
    if lat_count == 2:
        rows_in = lax.ppermute(outward[0], "lat", ring_perm(2, 1))
        corner = lon_pick(outward[1], 1)
        from_top, from_bottom = rows_in, rows_in
        edge = side + corner
    else:
        down_rows, down_edge, up_rows, up_edge = outward
        from_top = lax.ppermute(down_rows, "lat", ring_perm(lat_count, 1))
        from_bottom = lax.ppermute(up_rows, "lat", ring_perm(lat_count, -1))
        zero = jnp.zeros_like(side)
        edge = (
            side
            + jnp.where(has_top, lon_pick(down_edge, 1), zero)
            + jnp.where(has_bottom, lon_pick(up_edge, -1), zero)
        )
    from_top = jnp.where(has_top, from_top, jnp.zeros_like(from_top))
    from_bottom = jnp.where(has_bottom, from_bottom, jnp.zeros_like(from_bottom))
    own = jnp.concatenate([from_top[:REACH], state, from_bottom[:REACH], edge[:1]], axis=0)
    base_edge = jnp.concatenate([from_top[REACH:], from_bottom[REACH:], edge[1:]], axis=0)

    conv_weights, own = lax.optimization_barrier((conv_weights, own))
    lift, out_lanes = lane_weights(lift_weight, out_weight)
    conv_a, conv_b = pl.pallas_call(
        tap_kernel,
        out_shape=(shape((10 * LANES, 2 * LANES), BF),) * 2,
        in_specs=[vmem],
        out_specs=[vmem] * 2,
        compiler_params=pltpu.CompilerParams(vmem_limit_bytes=GRANT),
    )(conv_weights)
    tm_count = lax.axis_size("tm")

    def neighbours(array):
        prev = lax.ppermute(array, "tm", ring_perm(tm_count, 1))
        following = lax.ppermute(array, "tm", ring_perm(tm_count, -1))
        return prev, following

    geometry = (frames, chans, rows, ring, pad)

    def scratch(in_rows, *more):
        return [
            pltpu.VMEM((frames, in_rows // 2, pad, 5 * LANES), BF),
            pltpu.VMEM((frames, in_rows // 2 - 1, pad, 5 * LANES), BF),
            pltpu.VMEM((frames, in_rows, ring + 2 * GUARD, LANES), F32),
            pltpu.VMEM(((in_rows + 1) * LANES, 6 * fc), BF),
            pltpu.VMEM((2, LANES, 2 * LANES), F32),
            *more,
            pltpu.SMEM(step_sizes.shape, F32),
            pltpu.SemaphoreType.DMA,
            *[pltpu.VMEM((ring + 2 * GUARD, LANES), F32)] * SLABS,
        ]

    prev, following = neighbours(own)
    nxt, current = pl.pallas_call(
        functools.partial(first_kernel, geometry),
        out_shape=(shape((rows + 5, fc, cols), BF), shape((rows + 4, fc, cols), F32)),
        in_specs=[hbm] + [vmem] * 9,
        out_specs=[vmem] * 2,
        scratch_shapes=scratch(rows + 2 * REACH, pltpu.VMEM((2, frames, LANES, LANES), F32)),
        compiler_params=pltpu.CompilerParams(vmem_limit_bytes=GRANT),
    )(steps, own, prev, following, base, base_edge, lift, conv_a, conv_b, out_lanes)

    prev, following = neighbours(nxt)
    result = pl.pallas_call(
        functools.partial(last_kernel, geometry),
        out_shape=shape((fc * rows, cols), F32),
        in_specs=[hbm] + [vmem] * 11,
        out_specs=vmem,
        scratch_shapes=scratch(rows + 4),
        compiler_params=pltpu.CompilerParams(vmem_limit_bytes=GRANT),
    )(
        steps, nxt, prev, following, current, flat(observed), flat(obs_weight),
        noise_field.reshape(-1, cols), lift, conv_a, conv_b, out_lanes,
    )
    return result.reshape(prior_state.shape)


def solution(mesh):
    placed = (
        P(("groups", "tm"), None, "lat", "lon"),
        P(("groups", "tm"), None, "lat", "lon"),
        P(("groups", "tm"), None, "lat", "lon"),
        P(None, ("groups", "tm"), None, "lat", "lon"),
        P(),
        P(),
        P(),
        P(),
    )
    return jax.shard_map(
        per_device,
        mesh=mesh,
        in_specs=placed,
        out_specs=P(("groups", "tm"), None, "lat", "lon"),
        check_vma=False,
    )
```
